32 devices in a mesh: ctx: 8 (over y, x, core), dp: 4 (over z).
Axes of the slice: x: 2, y: 2, z: 4, core: 2. Of those that a mesh axis runs over, the one named last changes fastest.
Arguments:
- tokens: bfloat16 [4, 4096, 2048], P('dp', 'ctx'), may hold values from -6 to 6
- w_query: bfloat16 [2048, 1024], replicated, may hold values from -0.125 to 0.125
- w_key: bfloat16 [2048, 1024], replicated, may hold values from -0.125 to 0.125
- w_value: bfloat16 [2048, 1024], replicated, may hold values from -0.125 to 0.125
- cotangent: bfloat16 [4, 4096, 1024], P('dp', 'ctx'), may hold values from -6 to 6
Outputs:
- attn_out: bfloat16 [4, 4096, 1024], P('dp', 'ctx')
- input_grad: bfloat16 [4, 4096, 2048], P('dp', 'ctx')
- grad_query: float32 [2048, 1024], P(('ctx', 'dp'))
- grad_key: float32 [2048, 1024], P(('ctx', 'dp'))
- grad_value: float32 [2048, 1024], P(('ctx', 'dp'))
The draws below stay inside these ranges and needn't reach their ends.
All inputs are finite; a program needn't handle non-finite values.
Results may differ from the reference program's by a relative error of at most 0.022.
Values may be sent and summed in bfloat16 or wider, within the bound.
A program may use at most 192 MiB of HBM per device.

```python
import jax
import jax.numpy as jnp
from jax import lax

D = 2048
HEADS = 8
DH = 128
TOK_DEV = 512
SEQ = 4096
SEQS = 4
HD = 1024


def with_spikes(values, stream_key, source, target, shards_of, factor):
    owner, partner = [(jnp.arange(values.shape[dim]) // (values.shape[dim] // shards_of)).reshape([-1 if axis == dim else 1 for axis in range(values.ndim)]) for dim in (source, target)]
    chosen = jax.random.permutation(stream_key, shards_of)[partner]
    strong = (owner == chosen) | (owner == (partner + shards_of // 2) % shards_of)
    return jnp.where(strong, factor * values, values)


def shard_levels(rng, dims, cuts, smallest, largest):
    level = 1.0
    for axis_at, shards_of in cuts:
        draws = jax.random.uniform(jax.random.fold_in(jax.random.fold_in(rng, 6), axis_at), (shards_of,), jnp.float32, smallest / len(cuts), largest / len(cuts))
        level = level * jnp.repeat(jnp.exp(draws), dims[axis_at] // shards_of).reshape((-1,) + (1,) * (len(dims) - 1 - axis_at))
    return level


def noise(own_key, extent, scale, most, shards=(), kind=jnp.bfloat16):
    drawn = scale * jax.random.normal(own_key, extent, jnp.float32)
    if shards:
        drawn = drawn * shard_levels(own_key, extent, shards, -0.22, 0.18)
    return jnp.clip(drawn, -most, most).astype(kind)


def heavy_noise(rng, dims, deviation, limit, shards, heavy, kind=jnp.bfloat16):
    values = deviation * jax.random.normal(rng, dims, jnp.float32)
    if shards:
        values = values * shard_levels(rng, dims, shards, -0.22, 0.18)
    return jnp.clip(with_spikes(values, jax.random.fold_in(rng, 3), *heavy), -limit, limit).astype(kind)


def setup_inputs(seed: int = 0) -> dict:
    splits = jax.random.split(jax.random.key(seed), 6)
    tokens = heavy_noise(splits[0], (SEQS, SEQ, D), 1.0, 6.0, ((0, 4), (1, 8)), (1, 2, 8, 2.0))
    w_query = noise(splits[1], (D, HD), D ** -0.5, 0.125)
    w_key = noise(splits[2], (D, HD), D ** -0.5, 0.125)
    w_value = noise(splits[3], (D, HD), D ** -0.5, 0.125)
    cotangent = noise(splits[4], (SEQS, SEQ, HD), 1.0, 6.0, ((0, 4), (1, 8)))
    return {"tokens": tokens, "w_query": w_query, "w_key": w_key, "w_value": w_value, "cotangent": cotangent}


EPS = 1e-05

def round_trip(value):
    return lax.optimization_barrier(value.astype(jnp.bfloat16)).astype(jnp.float32)

def one_sequence(tokens, cotangent, w_query, w_key, w_value):
    blocks = SEQ // TOK_DEV
    query = jnp.dot(tokens, w_query, preferred_element_type=jnp.float32).astype(jnp.bfloat16)
    key = jnp.dot(tokens, w_key, preferred_element_type=jnp.float32).astype(jnp.bfloat16)
    value = jnp.dot(tokens, w_value, preferred_element_type=jnp.float32).astype(jnp.bfloat16)

    def split(array):
        return array.astype(jnp.float32).reshape(blocks, TOK_DEV, HEADS, DH)
    qb, kb, vb = (split(query), split(key), split(value))
    rows = jnp.arange(TOK_DEV, dtype=jnp.int32)
    causal = (rows[:, None] >= rows[None, :]).astype(jnp.float32)
    state = round_trip(jnp.einsum('ntha,nthb->nhab', kb, vb))
    zero_state = jnp.zeros((1, HEADS, DH, DH), jnp.float32)
    prefix = round_trip(jnp.concatenate([zero_state, jnp.cumsum(state, axis=0)[:-1]], axis=0))
    scores = round_trip(jnp.einsum('ntha,nsha->nhts', qb, kb) * causal)
    mixed = jnp.einsum('nhts,nshb->nthb', scores, vb) + jnp.einsum('ntha,nhab->nthb', qb, prefix)
    inverse = lax.rsqrt(lax.optimization_barrier(jnp.mean(mixed * mixed, axis=-1, keepdims=True)) + EPS)
    normed = mixed * inverse
    attn_out = normed.astype(jnp.bfloat16).reshape(SEQ, HEADS * DH)
    upstream = split(cotangent)
    grad_mixed = round_trip((upstream - normed * lax.optimization_barrier(jnp.mean(upstream * normed, axis=-1, keepdims=True))) * inverse)
    back = round_trip(jnp.einsum('ntha,nthb->nhab', qb, grad_mixed))
    later = jnp.cumsum(back[::-1], axis=0)[::-1]
    suffix = round_trip(jnp.concatenate([later[1:], zero_state], axis=0))
    grad_scores = round_trip(jnp.einsum('nthb,nshb->nhts', grad_mixed, vb) * causal)
    grad_q = jnp.einsum('nhts,nsha->ntha', grad_scores, kb) + jnp.einsum('nthb,nhab->ntha', grad_mixed, prefix)
    grad_k = jnp.einsum('nhts,ntha->nsha', grad_scores, qb) + jnp.einsum('nshb,nhab->nsha', vb, suffix)
    grad_v = jnp.einsum('nhts,nthb->nshb', scores, grad_mixed) + jnp.einsum('nsha,nhab->nshb', kb, suffix)
    grad_q = grad_q.astype(jnp.bfloat16).reshape(SEQ, HEADS * DH)
    grad_k = grad_k.astype(jnp.bfloat16).reshape(SEQ, HEADS * DH)
    grad_v = grad_v.astype(jnp.bfloat16).reshape(SEQ, HEADS * DH)
    input_grad = (jnp.dot(grad_q, w_query.T, preferred_element_type=jnp.float32) + jnp.dot(grad_k, w_key.T, preferred_element_type=jnp.float32) + jnp.dot(grad_v, w_value.T, preferred_element_type=jnp.float32)).astype(jnp.bfloat16)
    combined = jnp.concatenate([grad_q, grad_k, grad_v], axis=1)
    weights = jnp.dot(tokens.T, combined, preferred_element_type=jnp.float32)
    return (attn_out, input_grad, weights)

def reference(tokens, w_query, w_key, w_value, cotangent):

    def run(pair):
        return one_sequence(pair[0], pair[1], w_query, w_key, w_value)
    attn_out, input_grad, weights = lax.map(run, (tokens, cotangent))
    summed = lax.optimization_barrier(jnp.sum(weights, axis=0)) * float(SEQS * SEQ) ** (-0.5)
    width = HEADS * DH
    return (attn_out, input_grad, summed[:, :width], summed[:, width:2 * width], summed[:, 2 * width:])
```

```python
import jax
import jax.numpy as jnp
from jax import lax
from jax.sharding import PartitionSpec as P

HEADS = 8
DH = 128


EPS = 1e-05


def swap(x, bit, size):
    return lax.ppermute(x, "ctx", [(i, i ^ (1 << bit)) for i in range(size)])


def halves(x, axis, mine):
    keep = lax.dynamic_index_in_dim(x, mine, axis, keepdims=False)
    away = lax.dynamic_index_in_dim(x, 1 - mine, axis, keepdims=False)
    return keep, away


def scatter_bits(x, order, bits, position, size):
    left = sorted(order, reverse=True)
    for bit in order:
        keep, away = halves(x, left.index(bit), (position >> bit) & 1)
        left.remove(bit)
        got = swap(away, bit, size)
        x = (keep.astype(jnp.float32) + got.astype(jnp.float32)).astype(jnp.bfloat16)
    return x


def scatter_dp(x, dp_count):
    dp = lax.axis_index("dp")
    total = lax.dynamic_index_in_dim(x, dp, 0, keepdims=False).astype(jnp.float32)
    for shift in range(1, dp_count):
        part = lax.dynamic_index_in_dim(x, lax.rem(dp + shift, dp_count), 0, keepdims=False)
        got = lax.ppermute(part, "dp", [(i, (i + shift) % dp_count) for i in range(dp_count)])
        total = total + got.astype(jnp.float32)
    return total


def weight_grad(mine, other, grad, position, size, dp_count):
    bits = size.bit_length() - 1
    width = grad.shape[1]
    away = jnp.dot(other.T, grad, preferred_element_type=jnp.float32).astype(jnp.bfloat16)
    got = swap(away, 0, size)
    keep = jnp.dot(mine.T, grad, preferred_element_type=jnp.float32)
    keep = (keep + got.astype(jnp.float32)).astype(jnp.bfloat16)
    half = width // 2
    mid = 1 + (bits - 1) // 2
    orders = (
        list(range(1, bits)),
        list(range(mid, bits)) + list(range(1, mid)),
    )
    out = []
    for number, order in enumerate(orders):
        part = keep[:, number * half : (number + 1) * half]
        part = part.reshape([2] * (bits - 1) + [dp_count, -1, half])
        out.append(scatter_dp(scatter_bits(part, order, bits, position, size), dp_count))
    return jnp.concatenate(out, axis=1)


def per_device(tokens, w_query, w_key, w_value, cotangent):
    source = tokens[0]
    ctx_count = lax.axis_size("ctx")
    dp_count = lax.axis_size("dp")
    rows = source.shape[0]
    width = HEADS * DH
    key = (
        jnp.dot(source, w_key, preferred_element_type=jnp.float32)
        .astype(jnp.bfloat16)
        .reshape(rows, HEADS, DH)
    )
    value = (
        jnp.dot(source, w_value, preferred_element_type=jnp.float32)
        .astype(jnp.bfloat16)
        .reshape(rows, HEADS, DH)
    )
    position = lax.axis_index("ctx")
    local_state = jnp.einsum("tha,thb->hab", key, value, preferred_element_type=jnp.float32).astype(
        jnp.bfloat16
    )
    piece = lax.all_gather(local_state[None], "ctx", axis=0, tiled=True)
    source_q, local_state = lax.optimization_barrier((source, local_state))
    query = (
        jnp.dot(source_q, w_query, preferred_element_type=jnp.float32)
        .astype(jnp.bfloat16)
        .reshape(rows, HEADS, DH)
    )
    index = jnp.arange(rows, dtype=jnp.int32)
    causal = (index[:, None] >= index[None, :]).astype(jnp.float32)
    scores = (
        jnp.einsum("tha,sha->hts", query, key, preferred_element_type=jnp.float32) * causal
    ).astype(jnp.bfloat16)
    mixed = jnp.einsum("hts,shb->thb", scores, value, preferred_element_type=jnp.float32)
    piece, mixed = lax.optimization_barrier((piece, mixed))
    keep = (jnp.arange(piece.shape[0], dtype=jnp.int32) < position).astype(jnp.float32)
    prefix = jnp.einsum("n,nhab->hab", keep, piece.astype(jnp.float32))
    prefix = prefix.astype(jnp.bfloat16)
    mixed = mixed + jnp.einsum("tha,hab->thb", query, prefix, preferred_element_type=jnp.float32)
    inverse = lax.rsqrt(jnp.mean(mixed * mixed, axis=-1, keepdims=True) + EPS)
    normed = mixed * inverse
    attn_out = normed.astype(jnp.bfloat16).reshape(rows, width)
    upstream = cotangent[0].astype(jnp.float32).reshape(rows, HEADS, DH)
    grad_mixed = (
        (upstream - normed * jnp.mean(upstream * normed, axis=-1, keepdims=True)) * inverse
    ).astype(jnp.bfloat16)
    back_state = jnp.einsum(
        "tha,thb->hab", query, grad_mixed, preferred_element_type=jnp.float32
    ).astype(jnp.bfloat16)
    piece = lax.all_gather(back_state[None], "ctx", axis=0, tiled=True)
    grad_mixed, back_state = lax.optimization_barrier((grad_mixed, back_state))
    grad_scores = (
        jnp.einsum("thb,shb->hts", grad_mixed, value, preferred_element_type=jnp.float32) * causal
    ).astype(jnp.bfloat16)
    grad_q = jnp.einsum(
        "hts,sha->tha", grad_scores, key, preferred_element_type=jnp.float32
    ) + jnp.einsum("thb,hab->tha", grad_mixed, prefix, preferred_element_type=jnp.float32)
    grad_q = grad_q.astype(jnp.bfloat16).reshape(rows, width)
    columns = source.reshape(rows, ctx_count // 2, 2, -1)
    mine, other = halves(columns, 2, position & 1)
    mine, other = mine.reshape(rows, -1), other.reshape(rows, -1)
    args = (position, ctx_count, dp_count)
    sums = [weight_grad(mine, other, grad_q, *args)]
    piece, grad_q = lax.optimization_barrier((piece, grad_q))
    keep = (jnp.arange(piece.shape[0], dtype=jnp.int32) > position).astype(jnp.float32)
    suffix = jnp.einsum("n,nhab->hab", keep, piece.astype(jnp.float32))
    suffix = suffix.astype(jnp.bfloat16)
    grad_k = jnp.einsum(
        "hts,tha->sha", grad_scores, query, preferred_element_type=jnp.float32
    ) + jnp.einsum("shb,hab->sha", value, suffix, preferred_element_type=jnp.float32)
    grad_v = jnp.einsum(
        "hts,thb->shb", scores, grad_mixed, preferred_element_type=jnp.float32
    ) + jnp.einsum("sha,hab->shb", key, suffix, preferred_element_type=jnp.float32)
    grad_k = grad_k.astype(jnp.bfloat16).reshape(rows, width)
    grad_v = grad_v.astype(jnp.bfloat16).reshape(rows, width)
    for grad in (grad_k, grad_v):
        sums.append(weight_grad(mine, other, grad, *args))
    input_grad = (
        jnp.dot(grad_q, w_query.T, preferred_element_type=jnp.float32)
        + jnp.dot(grad_k, w_key.T, preferred_element_type=jnp.float32)
        + jnp.dot(grad_v, w_value.T, preferred_element_type=jnp.float32)
    ).astype(jnp.bfloat16)
    scale = float(rows * ctx_count * dp_count) ** (-0.5)
    return (attn_out[None], input_grad[None], *[total * scale for total in sums])


def solution(mesh):
    return jax.shard_map(
        per_device,
        mesh=mesh,
        in_specs=(P("dp", "ctx", None), P(), P(), P(), P("dp", "ctx", None)),
        out_specs=(
            P("dp", "ctx", None),
            P("dp", "ctx", None),
            P(("ctx", "dp"), None),
            P(("ctx", "dp"), None),
            P(("ctx", "dp"), None),
        ),
        check_vma=False,
    )
```

```python
import jax
import jax.numpy as jnp
from jax import lax
from jax.experimental import pallas as pl
from jax.experimental.pallas import tpu as pltpu
from jax.sharding import PartitionSpec as P

HEADS = 8
DH = 128


EPS = 1e-05


def swap(x, bit, size):
    return lax.ppermute(x, "ctx", [(i, i ^ (1 << bit)) for i in range(size)])


def halves(x, axis, mine):
    keep = lax.dynamic_index_in_dim(x, mine, axis, keepdims=False)
    away = lax.dynamic_index_in_dim(x, 1 - mine, axis, keepdims=False)
    return keep, away


def scatter_bits(x, order, bits, position, size):
    left = sorted(order, reverse=True)
    for bit in order:
        keep, away = halves(x, left.index(bit), (position >> bit) & 1)
        left.remove(bit)
        got = swap(away, bit, size)
        x = (keep.astype(jnp.float32) + got.astype(jnp.float32)).astype(jnp.bfloat16)
    return x


def scatter_dp(x, dp_count):
    dp = lax.axis_index("dp")
    total = lax.dynamic_index_in_dim(x, dp, 0, keepdims=False).astype(jnp.float32)
    for shift in range(1, dp_count):
        part = lax.dynamic_index_in_dim(x, lax.rem(dp + shift, dp_count), 0, keepdims=False)
        got = lax.ppermute(part, "dp", [(i, (i + shift) % dp_count) for i in range(dp_count)])
        total = total + got.astype(jnp.float32)
    return total


def chip_grad(mine, other, grad, size):
    away = jnp.dot(other.T, grad, preferred_element_type=jnp.float32).astype(jnp.bfloat16)
    got = swap(away, 0, size)
    keep = jnp.dot(mine.T, grad, preferred_element_type=jnp.float32)
    return (keep + got.astype(jnp.float32)).astype(jnp.bfloat16)


def rest_grad(keep, position, size, dp_count):
    bits = size.bit_length() - 1
    half = keep.shape[1] // 2
    mid = 1 + (bits - 1) // 2
    orders = (
        list(range(1, bits)),
        list(range(mid, bits)) + list(range(1, mid)),
    )
    out = []
    for number, order in enumerate(orders):
        part = keep[:, number * half : (number + 1) * half]
        part = part.reshape([2] * (bits - 1) + [dp_count, -1, half])
        out.append(scatter_bits(part, order, bits, position, size))
    return scatter_dp(jnp.concatenate(out, axis=2), dp_count)


def mm(a, b, ca, cb):
    return lax.dot_general(a, b, (((ca,), (cb,)), ((), ())), preferred_element_type=jnp.float32)


def masked(x, lower):
    row = lax.broadcasted_iota(jnp.int32, x.shape, 0)
    col = lax.broadcasted_iota(jnp.int32, x.shape, 1)
    keep = row >= col if lower else row <= col
    return jnp.where(keep, x, 0.0).astype(jnp.bfloat16)


def state_kernel(k, v, state):
    state[0] = mm(k[...], v[...], 0, 0).astype(jnp.bfloat16)


def intra_kernel(q, k, v, out):
    scores = masked(mm(q[...], k[...], 1, 1), True)
    out[...] = mm(scores, v[...], 1, 0)


def weighted(keep, piece):
    total = keep[0] * piece[0, 0].astype(jnp.float32)
    for n in range(1, piece.shape[0]):
        total = total + keep[n] * piece[n, 0].astype(jnp.float32)
    return total.astype(jnp.bfloat16)


def norm_kernel(keep, piece, q, intra, cot, attn, grad, prefix, back):
    before = weighted(keep, piece)
    prefix[0] = before
    mixed = intra[...] + mm(q[...], before, 1, 0)
    inverse = lax.rsqrt(jnp.mean(mixed * mixed, axis=-1, keepdims=True) + EPS)
    normed = mixed * inverse
    attn[...] = normed.astype(jnp.bfloat16)
    upstream = cot[...].astype(jnp.float32)
    inner = jnp.mean(upstream * normed, axis=-1, keepdims=True)
    gm = ((upstream - normed * inner) * inverse).astype(jnp.bfloat16)
    grad[...] = gm
    back[0] = mm(q[...], gm, 0, 0).astype(jnp.bfloat16)


def back_kernel(q, k, v, grad, prefix, dq, dk, dv):
    gm = grad[...]
    gs = masked(mm(gm, v[...], 1, 1), True)
    dq[...] = (mm(gs, k[...], 1, 0) + mm(gm, prefix[0], 1, 1)).astype(jnp.bfloat16)
    gst = masked(mm(v[...], gm, 1, 1), False)
    dk[...] = mm(gst, q[...], 1, 0)
    st = masked(mm(k[...], q[...], 1, 1), False)
    dv[...] = mm(st, gm, 1, 0)


def suffix_kernel(keep, piece, k, v, dk0, dv0, dk, dv):
    after = weighted(keep, piece)
    dk[...] = (dk0[...] + mm(v[...], after, 1, 1)).astype(jnp.bfloat16)
    dv[...] = (dv0[...] + mm(k[...], after, 1, 0)).astype(jnp.bfloat16)


def by_head(kernel, ins, outs, rows, flops, name):
    def spec(shape):
        if len(shape) == 1:
            return pl.BlockSpec(memory_space=pltpu.SMEM)
        if len(shape) == 2:
            return pl.BlockSpec((rows, DH), lambda h: (0, h))
        if len(shape) == 3:
            return pl.BlockSpec((1, DH, DH), lambda h: (h, 0, 0))
        return pl.BlockSpec((shape[0], 1, DH, DH), lambda h: (0, h, 0, 0))

    out_shape = [
        jax.ShapeDtypeStruct((HEADS, DH, DH), jnp.bfloat16)
        if kind == "state"
        else jax.ShapeDtypeStruct((rows, HEADS * DH), kind)
        for kind in outs
    ]
    nbytes = sum(a.size * a.dtype.itemsize for a in list(ins) + out_shape)
    return pl.pallas_call(
        kernel,
        grid=(HEADS,),
        in_specs=[spec(a.shape) for a in ins],
        out_specs=[spec(o.shape) for o in out_shape],
        out_shape=out_shape,
        name=name,
        cost_estimate=pl.CostEstimate(
            flops=2 * rows * DH * DH * HEADS * flops, bytes_accessed=nbytes, transcendentals=0
        ),
    )(*ins)


def per_device(tokens, w_query, w_key, w_value, cotangent):
    source = tokens[0]
    ctx_count = lax.axis_size("ctx")
    dp_count = lax.axis_size("dp")
    rows = source.shape[0]
    bf = jnp.bfloat16
    position = lax.axis_index("ctx")
    block = jnp.arange(ctx_count, dtype=jnp.int32)
    key = jnp.dot(source, w_key, preferred_element_type=jnp.float32).astype(bf)
    value = jnp.dot(source, w_value, preferred_element_type=jnp.float32).astype(bf)
    (local_state,) = by_head(state_kernel, (key, value), ("state",), rows, 1, "state")
    piece = lax.all_gather(local_state[None], "ctx", axis=0, tiled=True)
    source_q, local_state = lax.optimization_barrier((source, local_state))
    query = jnp.dot(source_q, w_query, preferred_element_type=jnp.float32).astype(bf)
    (intra,) = by_head(intra_kernel, (query, key, value), (jnp.float32,), rows, 8, "intra")
    columns = source_q.reshape(rows, ctx_count // 2, 2, -1)
    mine, other = halves(columns, 2, position & 1)
    mine, other = mine.reshape(rows, -1), other.reshape(rows, -1)
    piece, intra, mine, other = lax.optimization_barrier((piece, intra, mine, other))
    keep = (block < position).astype(jnp.float32)
    attn_out, grad_mixed, prefix, back_state = by_head(
        norm_kernel,
        (keep, piece, query, intra, cotangent[0]),
        (bf, bf, "state", "state"),
        rows,
        3,
        "norm",
    )
    piece = lax.all_gather(back_state[None], "ctx", axis=0, tiled=True)
    grad_q, part_k, part_v = by_head(
        back_kernel,
        (query, key, value, grad_mixed, prefix),
        (bf, jnp.float32, jnp.float32),
        rows,
        25,
        "back",
    )
    args = (position, ctx_count, dp_count)
    chip_q = chip_grad(mine, other, grad_q, ctx_count)
    piece, chip_q = lax.optimization_barrier((piece, chip_q))
    sum_q = rest_grad(chip_q, *args)
    keep = (block > position).astype(jnp.float32)
    grad_k, grad_v = by_head(
        suffix_kernel, (keep, piece, key, value, part_k, part_v), (bf, bf), rows, 2, "suffix"
    )
    chip_k, chip_v = [chip_grad(mine, other, grad, ctx_count) for grad in (grad_k, grad_v)]
    sum_k, sum_v = rest_grad(chip_k, *args), rest_grad(chip_v, *args)
    grad_q, grad_k, grad_v, _ = lax.optimization_barrier((grad_q, grad_k, grad_v, chip_v))
    input_grad = (
        jnp.dot(grad_q, w_query.T, preferred_element_type=jnp.float32)
        + jnp.dot(grad_k, w_key.T, preferred_element_type=jnp.float32)
        + jnp.dot(grad_v, w_value.T, preferred_element_type=jnp.float32)
    ).astype(bf)
    scale = float(rows * ctx_count * dp_count) ** (-0.5)
    return (attn_out[None], input_grad[None], sum_q * scale, sum_k * scale, sum_v * scale)


def solution(mesh):
    return jax.shard_map(
        per_device,
        mesh=mesh,
        in_specs=(P("dp", "ctx", None), P(), P(), P(), P("dp", "ctx", None)),
        out_specs=(
            P("dp", "ctx", None),
            P("dp", "ctx", None),
            P(("ctx", "dp"), None),
            P(("ctx", "dp"), None),
            P(("ctx", "dp"), None),
        ),
        check_vma=False,
    )
```
